32 devices in a mesh: expert: 8 (over z, core), hidden: 4 (over y, x).
Axes of the slice: x: 2, y: 2, z: 4, core: 2. Of those that a mesh axis runs over, the one named last changes fastest.
Arguments:
- inputs: bfloat16 [32768, 768], P(('expert', 'hidden')), may hold values from -6 to 6
- out_grad: bfloat16 [32768, 768], P(('expert', 'hidden')), may hold values from -6 to 6
- seq_lengths: int32 [32], P(('expert', 'hidden')), may hold values from 1 to 1024, 16384 in all
- routes: int32 [32768, 2], P(('expert', 'hidden')), may hold values from 0 to 15, all different within a row
- norm_master: float32 [4, 768], P(None, ('expert', 'hidden')), may hold values from 0.25 to 1.75
- norm_momentum: float32 [4, 768], P(None, ('expert', 'hidden')), may hold values from -768 to 768
- norm_average: float32 [4, 768], P(None, ('expert', 'hidden')), may hold values from 0.25 to 1.75
- qkv_master: float32 [768, 2304], P(('expert', 'hidden')), may hold values from -0.21875 to 0.21875
- qkv_momentum: float32 [768, 2304], P(('expert', 'hidden')), may hold values from -512 to 512
- qkv_average: float32 [768, 2304], P(('expert', 'hidden')), may hold values from -0.21875 to 0.21875
- proj_master: float32 [768, 768], P(None, ('expert', 'hidden')), may hold values from -1.75 to 1.75
- proj_momentum: float32 [768, 768], P(None, ('expert', 'hidden')), may hold values from -112 to 112
- proj_average: float32 [768, 768], P(None, ('expert', 'hidden')), may hold values from -1.75 to 1.75
- router_master: float32 [768, 16], P(('expert', 'hidden')), may hold values from -0.21875 to 0.21875
- router_momentum: float32 [768, 16], P(('expert', 'hidden')), may hold values from -1536 to 1536
- router_average: float32 [768, 16], P(('expert', 'hidden')), may hold values from -0.21875 to 0.21875
- frozen_in: bfloat16 [8, 768, 3072], P('expert', None, 'hidden'), may hold values from -0.21875 to 0.21875
- frozen_out: bfloat16 [8, 3072, 768], P('expert', 'hidden'), may hold values from -0.109375 to 0.109375
- expert_in_master: float32 [8, 768, 3072], P('expert', None, 'hidden'), may hold values from -0.21875 to 0.21875
- expert_in_momentum: float32 [8, 768, 3072], P('expert', None, 'hidden'), may hold values from -28 to 28
- expert_in_average: float32 [8, 768, 3072], P('expert', None, 'hidden'), may hold values from -0.21875 to 0.21875
- expert_out_master: float32 [8, 3072, 768], P('expert', 'hidden'), may hold values from -0.109375 to 0.109375
- expert_out_momentum: float32 [8, 3072, 768], P('expert', 'hidden'), may hold values from -56 to 56
- expert_out_average: float32 [8, 3072, 768], P('expert', 'hidden'), may hold values from -0.109375 to 0.109375
Outputs:
- outputs: bfloat16 [32768, 768], P(('expert', 'hidden'))
- input_grad: float32 [32768, 768], P(('expert', 'hidden'))
- norm_grad: float32 [4, 768], P(None, ('expert', 'hidden'))
- norm_moment: float32 [4, 768], P(None, ('expert', 'hidden'))
- norm_weight: float32 [4, 768], P(None, ('expert', 'hidden'))
- norm_ema: float32 [4, 768], P(None, ('expert', 'hidden'))
- qkv_grad: float32 [768, 2304], P(('expert', 'hidden'))
- qkv_moment: float32 [768, 2304], P(('expert', 'hidden'))
- qkv_weight: float32 [768, 2304], P(('expert', 'hidden'))
- qkv_ema: float32 [768, 2304], P(('expert', 'hidden'))
- proj_grad: float32 [768, 768], P(None, ('expert', 'hidden'))
- proj_moment: float32 [768, 768], P(None, ('expert', 'hidden'))
- proj_weight: float32 [768, 768], P(None, ('expert', 'hidden'))
- proj_ema: float32 [768, 768], P(None, ('expert', 'hidden'))
- router_grad: float32 [768, 16], P(('expert', 'hidden'))
- router_moment: float32 [768, 16], P(('expert', 'hidden'))
- router_weight: float32 [768, 16], P(('expert', 'hidden'))
- router_ema: float32 [768, 16], P(('expert', 'hidden'))
- expert_in_grad: float32 [8, 768, 3072], P('expert', None, 'hidden')
- expert_in_moment: float32 [8, 768, 3072], P('expert', None, 'hidden')
- expert_in_weight: float32 [8, 768, 3072], P('expert', None, 'hidden')
- expert_in_ema: float32 [8, 768, 3072], P('expert', None, 'hidden')
- expert_out_grad: float32 [8, 3072, 768], P('expert', 'hidden')
- expert_out_moment: float32 [8, 3072, 768], P('expert', 'hidden')
- expert_out_weight: float32 [8, 3072, 768], P('expert', 'hidden')
- expert_out_ema: float32 [8, 3072, 768], P('expert', 'hidden')
The draws below stay inside these ranges and needn't reach their ends.
Inputs may be any that keep to these rules, and one draw needn't show every extreme that they name: `seq_lengths`: the longest sequence has exactly 1024 tokens and the lengths sum to 16384. `routes`: the two experts of a token differ, and every expert is named by some token.
All inputs are finite; a program needn't handle non-finite values. No bound on the sum of `seq_lengths` on one device may be relied on, other than what follows from the above.
Results may differ from the reference program's by a relative error of at most 0.015.
The reference program's roundings to bfloat16 on the way count: a program that leaves them out, or rounds other values in their place, can miss the bound.
Values may be sent and summed in bfloat16 or wider, within the bound.
No kernel may reach another device: no remote copies, remote signals or barrier semaphores. Data moves between devices by JAX's collectives and lax.ppermute only.
A program may use at most 320 MiB of HBM per device.

```python
import math
import jax
import jax.numpy as jnp
import numpy as np
from jax import lax

D = 768
HEADS = 12
HEAD_DIM = 64
FF = 3072
TOP = 2
SEQ_LEN = 1024
TOK_DEV = 1024
SEQS = 32
TOKENS = 32768
EXPERTS = 16
CAP = 64
DEVICES = 32


def spiked(array, key, source, target, blocks, factor):
    owner, partner = [(jnp.arange(array.shape[dim]) // (array.shape[dim] // blocks)).reshape([-1 if axis == dim else 1 for axis in range(array.ndim)]) for dim in (source, target)]
    chosen = jax.random.permutation(key, blocks)[partner]
    strong = (owner == chosen) | (owner == (partner + blocks // 2) % blocks)
    return jnp.where(strong, factor * array, array)


def levels(stream_key, shape, split, low, largest):
    gain = 1.0
    for position, blocks in split:
        heights = jax.random.uniform(jax.random.fold_in(jax.random.fold_in(stream_key, 6), position), (blocks,), jnp.float32, low / len(split), largest / len(split))
        gain = gain * jnp.repeat(jnp.exp(heights), shape[position] // blocks).reshape((-1,) + (1,) * (len(shape) - 1 - position))
    return gain


def distinct(own_key, rows, count, top, lift):
    order = jax.random.permutation(jax.random.fold_in(own_key, 1), count)
    pull = order
    for power in range(3):
        pull = pull * pull // count
    pull = pull * lift // count
    tickets = jax.random.randint(jax.random.fold_in(own_key, 2), (rows, count), 0, 4096) + pull
    fixed_rows = jax.random.permutation(jax.random.fold_in(own_key, 3), rows)[jnp.arange(count) % rows]
    tickets = jnp.where(jnp.arange(rows)[:, None] == fixed_rows[None, :], 1 << 14, tickets)
    score = tickets * count + jnp.arange(count)
    return lax.top_k(score.astype(jnp.int32), top)[1].astype(jnp.int32)


def profile(count, total, limit, slope):
    portions = [(1 << 20) // math.isqrt(grade ** slope) + 1 for grade in range(2, count + 1)]
    spare, holding = total - limit - (count - 1), [1] * (count - 1)
    while spare > 0:
        candidates = [i for i in range(count - 1) if holding[i] < limit]
        whole, budget = sum([portions[i] for i in candidates]), spare
        for i in candidates:
            addition = min(limit - holding[i], max(1, budget * portions[i] // whole), spare)
            holding[i] = holding[i] + addition
            spare = spare - addition
    return np.array([limit] + holding)


def ragged(stream_key, amount, total, reach, skew):
    if amount == 2:
        one = jax.random.randint(stream_key, (), max(1, total - reach), min(reach, total - 1) + 1)
        return jnp.stack([one, total - one])
    lengths = jnp.asarray(profile(amount, total, reach, skew), jnp.int32)
    pairs = (amount - 1) // 2
    giver, receiver = lengths[1:1 + 2 * pairs:2], lengths[2:2 + 2 * pairs:2]
    room = jnp.minimum(giver - 1, reach - receiver)
    passed = jax.random.randint(jax.random.fold_in(stream_key, 1), (pairs,), 0, 1 << 20) % (room + 1)
    lengths = lengths.at[1:1 + 2 * pairs:2].set(giver - passed).at[2:2 + 2 * pairs:2].set(receiver + passed)
    return lengths[jax.random.permutation(jax.random.fold_in(stream_key, 2), amount)]


def centred(rng, extent, deviation, limit, split=(), kind=jnp.bfloat16):
    array = deviation * jax.random.normal(rng, extent, jnp.float32)
    if split:
        array = array * levels(rng, extent, split, -0.22, 0.18)
    return jnp.clip(array, -limit, limit).astype(kind)


def gaussian_with(own_key, extent, spread, limit, shards, heavy, held_as=jnp.bfloat16):
    drawn = spread * jax.random.normal(own_key, extent, jnp.float32)
    if shards:
        drawn = drawn * levels(own_key, extent, shards, -0.22, 0.18)
    return jnp.clip(spiked(drawn, jax.random.fold_in(own_key, 3), *heavy), -limit, limit).astype(held_as)


def setup_inputs(seed: int = 0) -> dict:
    arg_keys = jax.random.split(jax.random.key(seed), 25)
    inputs = centred(arg_keys[0], (TOKENS, D), 1.0, 6.0, ((0, 32),))
    out_grad = gaussian_with(arg_keys[1], (TOKENS, D), 1.0, 6.0, ((0, 32),), (0, 1, 32, 2.75))
    seq_lengths = ragged(arg_keys[2], SEQS, SEQS * SEQ_LEN // 2, SEQ_LEN, 2).astype(jnp.int32)
    routes = distinct(arg_keys[3], TOKENS, EXPERTS, TOP, 2048)
    norm_master = jnp.clip(1.0 + 0.15 * jax.random.normal(arg_keys[4], (4, D), jnp.float32), 0.25, 1.75)
    norm_momentum = centred(arg_keys[5], (4, D), (0.7 * TOKENS ** 0.5), 768.0, ((1, 32),), jnp.float32)
    norm_average = jnp.clip(1.0 + 0.15 * jax.random.normal(arg_keys[6], (4, D), jnp.float32), 0.25, 1.75)
    qkv_master = centred(arg_keys[7], (D, 3 * D), D ** -0.5, 0.21875, ((0, 32),), jnp.float32)
    qkv_momentum = centred(arg_keys[8], (D, 3 * D), (0.5 * TOKENS ** 0.5), 512.0, ((0, 32),), jnp.float32)
    qkv_average = centred(arg_keys[9], (D, 3 * D), D ** -0.5, 0.21875, ((0, 32),), jnp.float32)
    proj_master = centred(arg_keys[10], (D, D), (D // 64) ** -0.5, 1.75, ((1, 32),), jnp.float32)
    proj_momentum = centred(arg_keys[11], (D, D), (0.1 * TOKENS ** 0.5), 112.0, ((1, 32),), jnp.float32)
    proj_average = centred(arg_keys[12], (D, D), (D // 64) ** -0.5, 1.75, ((1, 32),), jnp.float32)
    router_master = centred(arg_keys[13], (D, EXPERTS), D ** -0.5, 0.21875, ((0, 32),), jnp.float32)
    router_momentum = centred(arg_keys[14], (D, EXPERTS), (6 * (TOKENS / EXPERTS) ** 0.5), 1536.0, ((0, 32),), jnp.float32)
    router_average = centred(arg_keys[15], (D, EXPERTS), D ** -0.5, 0.21875, ((0, 32),), jnp.float32)
    frozen_in = centred(arg_keys[16], (EXPERTS // 2, D, FF), D ** -0.5, 0.21875, ((0, 8), (2, 4)))
    frozen_out = centred(arg_keys[17], (EXPERTS // 2, FF, D), FF ** -0.5, 0.109375, ((0, 8), (1, 4)))
    expert_in_master = centred(arg_keys[18], (EXPERTS // 2, D, FF), D ** -0.5, 0.21875, ((0, 8), (2, 4)), jnp.float32)
    expert_in_momentum = centred(arg_keys[19], (EXPERTS // 2, D, FF), (0.1 * (TOKENS / EXPERTS) ** 0.5), 28.0, ((0, 8), (2, 4)), jnp.float32)
    expert_in_average = centred(arg_keys[20], (EXPERTS // 2, D, FF), D ** -0.5, 0.21875, ((0, 8), (2, 4)), jnp.float32)
    expert_out_master = centred(arg_keys[21], (EXPERTS // 2, FF, D), FF ** -0.5, 0.109375, ((0, 8), (1, 4)), jnp.float32)
    expert_out_momentum = centred(arg_keys[22], (EXPERTS // 2, FF, D), (0.2 * (TOKENS / EXPERTS) ** 0.5), 56.0, ((0, 8), (1, 4)), jnp.float32)
    expert_out_average = centred(arg_keys[23], (EXPERTS // 2, FF, D), FF ** -0.5, 0.109375, ((0, 8), (1, 4)), jnp.float32)
    return {"inputs": inputs, "out_grad": out_grad, "seq_lengths": seq_lengths, "routes": routes, "norm_master": norm_master, "norm_momentum": norm_momentum, "norm_average": norm_average, "qkv_master": qkv_master, "qkv_momentum": qkv_momentum, "qkv_average": qkv_average, "proj_master": proj_master, "proj_momentum": proj_momentum, "proj_average": proj_average, "router_master": router_master, "router_momentum": router_momentum, "router_average": router_average, "frozen_in": frozen_in, "frozen_out": frozen_out, "expert_in_master": expert_in_master, "expert_in_momentum": expert_in_momentum, "expert_in_average": expert_in_average, "expert_out_master": expert_out_master, "expert_out_momentum": expert_out_momentum, "expert_out_average": expert_out_average}


@jax.custom_vjp
def low(v):
    return lax.optimization_barrier(v.astype(jnp.bfloat16)).astype(jnp.float32)

@jax.custom_vjp
def low_back(v):
    return v

def low_keep(v):
    return (low(v), None)

def low_pass(kept, grad):
    return (grad,)

def back_keep(v):
    return (v, None)

def back_low(kept, grad):
    return (low(grad),)
low.defvjp(low_keep, low_pass)
low_back.defvjp(back_keep, back_low)
EPSILON = 1e-05
MOMENT = 0.9
KEEP_MEAN = 0.75
MASKED = -1e+30
PRECISE = lax.Precision.HIGHEST

def matmul(left, right):
    return jnp.dot(left, right, precision=PRECISE, preferred_element_type=jnp.float32)

def layer_norm(values, gain_row, shift_row):
    row_mean = lax.optimization_barrier(jnp.mean(values, axis=-1, keepdims=True))
    centered = values - row_mean
    inverse = lax.rsqrt(lax.optimization_barrier(jnp.mean(centered * centered, axis=-1, keepdims=True)) + EPSILON)
    return centered * inverse * gain_row + shift_row

def attend(queries, key_rows, value_rows, length):
    seq_pos = jnp.arange(SEQ_LEN, dtype=jnp.int32)
    scores = jnp.einsum('qhd,khd->hqk', queries, key_rows, precision=PRECISE) * HEAD_DIM ** (-0.5)
    scores = low_back(scores)
    allowed = (seq_pos[None, :] <= seq_pos[:, None]) & (seq_pos[None, :] < length)
    scores = jnp.where(allowed[None], scores, MASKED)
    probabilities = jax.nn.softmax(scores, axis=-1)
    return jnp.einsum('hqk,khd->qhd', low(probabilities), value_rows, precision=PRECISE)

def front(resid_group, length_group, norm_rows, w_qkv, w_proj, w_router):
    row_total = resid_group.shape[0]
    group_size = length_group.shape[0]
    attn_in = low(layer_norm(resid_group, norm_rows[0], norm_rows[1]))
    qkv_rows = low(low_back(matmul(attn_in, w_qkv)))
    shaped = qkv_rows.reshape(group_size, SEQ_LEN, 3, HEADS, HEAD_DIM)
    mixed = jax.vmap(attend)(shaped[:, :, 0], shaped[:, :, 1], shaped[:, :, 2], length_group)
    attn_out = low(low_back(mixed.reshape(row_total, D)))
    resid_mid = resid_group + low_back(matmul(attn_out, w_proj))
    moe_in = low(layer_norm(resid_mid, norm_rows[2], norm_rows[3]))
    logits = low_back(matmul(moe_in, w_router))
    return (resid_mid, moe_in, logits)

def expert_apply(padded_in, weight_in, weight_out, slot_token):
    slot_in = low_back(padded_in[slot_token])
    pre_act = low_back(matmul(slot_in, weight_in))
    activation = low(jax.nn.gelu(pre_act))
    return low(low_back(matmul(activation, weight_out)))

def nesterov(master, momentum, average, grad_full, rate):
    moment_new = MOMENT * momentum + grad_full
    weight_new = master - rate * (grad_full + MOMENT * moment_new)
    return (grad_full, moment_new, weight_new, KEEP_MEAN * average + (1.0 - KEEP_MEAN) * weight_new)

def reference(inputs, out_grad, seq_lengths, routes, norm_master, norm_momentum, norm_average, qkv_master, qkv_momentum, qkv_average, proj_master, proj_momentum, proj_average, router_master, router_momentum, router_average, frozen_in, frozen_out, expert_in_master, expert_in_momentum, expert_in_average, expert_out_master, expert_out_momentum, expert_out_average):
    group_size = math.gcd(SEQS, max(1, 4096 // SEQ_LEN))
    group_count = SEQS // group_size
    row_ids = jnp.arange(TOKENS, dtype=jnp.int32)
    row_length = jnp.repeat(seq_lengths, SEQ_LEN, total_repeat_length=TOKENS)
    live_rows = row_ids % SEQ_LEN < row_length
    live_float = live_rows.astype(jnp.float32)
    block_routes = routes.reshape(DEVICES, 2 * TOK_DEV)
    pair_live = jnp.repeat(live_rows, 2).reshape(DEVICES, 2 * TOK_DEV)
    expert_ids = jnp.arange(EXPERTS, dtype=jnp.int32)
    onehot = ((block_routes[:, :, None] == expert_ids[None, None, :]) & pair_live[:, :, None]).astype(jnp.int32)
    pair_rank = lax.optimization_barrier(jnp.sum((jnp.cumsum(onehot, axis=1) - onehot) * onehot, axis=2)).astype(jnp.int32)
    kept_pair = pair_live & (pair_rank < CAP)
    device_ids = jnp.arange(DEVICES, dtype=jnp.int32)[:, None]
    pair_token = (device_ids * TOK_DEV + jnp.arange(2 * TOK_DEV, dtype=jnp.int32)[None, :] // 2).astype(jnp.int32)
    slot_rows = DEVICES * CAP
    slot_flat = (block_routes * slot_rows + device_ids * CAP + jnp.minimum(pair_rank, CAP - 1)).astype(jnp.int32)
    slot_total = EXPERTS * slot_rows
    target = jnp.where(kept_pair, slot_flat, slot_total).reshape(-1).astype(jnp.int32)
    slot_token = jnp.full((slot_total + 1,), TOKENS, jnp.int32).at[target].set(pair_token.reshape(-1))
    slot_token = slot_token[:slot_total].reshape(EXPERTS, slot_rows)
    pair_slot = slot_flat.reshape(TOKENS, 2)
    kept_float = kept_pair.reshape(TOKENS, 2).astype(jnp.float32)
    frozen_in_full = frozen_in.astype(jnp.float32)
    frozen_out_full = frozen_out.astype(jnp.float32)

    def forward(resid_all, norm_param, qkv_param, proj_param, router_param, in_param, out_param):
        norm_rows = low(norm_param)
        w_qkv = low(qkv_param)
        w_proj = low(proj_param)
        w_router = low(router_param)

        def group_apply(items):
            return front(items[0], items[1], norm_rows, w_qkv, w_proj, w_router)
        resid_mid, moe_in, logits = lax.map(jax.checkpoint(group_apply), (resid_all.reshape(group_count, group_size * SEQ_LEN, D), seq_lengths.reshape(group_count, group_size)))
        resid_mid = resid_mid.reshape(TOKENS, D)
        moe_in = moe_in.reshape(TOKENS, D)
        logits = logits.reshape(TOKENS, EXPERTS)
        padded_in = jnp.concatenate([moe_in, jnp.zeros((1, D), jnp.float32)], axis=0)
        all_in = jnp.stack([frozen_in_full, low(in_param)], axis=1).reshape(EXPERTS, D, FF)
        all_out = jnp.stack([frozen_out_full, low(out_param)], axis=1).reshape(EXPERTS, FF, D)

        def expert_step(items):
            return expert_apply(padded_in, items[0], items[1], items[2])
        expert_rows = lax.map(jax.checkpoint(expert_step), (all_in, all_out, slot_token))
        expert_rows = expert_rows.reshape(EXPERTS * slot_rows, D)
        gates = jax.nn.softmax(jnp.take_along_axis(logits, routes, axis=1), axis=-1) * kept_float
        moe_out = expert_rows[pair_slot[:, 0]] * gates[:, 0:1] + expert_rows[pair_slot[:, 1]] * gates[:, 1:2]
        return live_float[:, None] * (resid_mid + moe_out)
    primal, pullback = jax.vjp(forward, inputs.astype(jnp.float32), norm_master, qkv_master, proj_master, router_master, expert_in_master, expert_out_master)
    grads = pullback(out_grad.astype(jnp.float32))
    outputs = primal.astype(jnp.bfloat16)
    input_grad = grads[0]
    norm_rate = 0.1 / math.sqrt(TOKENS)
    qkv_rate = 1.0 / math.sqrt(D * TOKENS)
    proj_rate = 40.0 / math.sqrt(D * TOKENS)
    router_rate = 0.08 * math.sqrt(EXPERTS / (D * TOKENS))
    in_rate = 5.0 * math.sqrt(EXPERTS / (D * TOKENS))
    out_rate = 2.5 * math.sqrt(EXPERTS / (FF * TOKENS))
    norm_set = nesterov(norm_master, norm_momentum, norm_average, grads[1], norm_rate)
    qkv_set = nesterov(qkv_master, qkv_momentum, qkv_average, grads[2], qkv_rate)
    proj_set = nesterov(proj_master, proj_momentum, proj_average, grads[3], proj_rate)
    router_set = nesterov(router_master, router_momentum, router_average, grads[4], router_rate)
    in_set = nesterov(expert_in_master, expert_in_momentum, expert_in_average, grads[5], in_rate)
    out_set = nesterov(expert_out_master, expert_out_momentum, expert_out_average, grads[6], out_rate)
    return (outputs, input_grad, norm_set[0], norm_set[1], norm_set[2], norm_set[3], qkv_set[0], qkv_set[1], qkv_set[2], qkv_set[3], proj_set[0], proj_set[1], proj_set[2], proj_set[3], router_set[0], router_set[1], router_set[2], router_set[3], in_set[0], in_set[1], in_set[2], in_set[3], out_set[0], out_set[1], out_set[2], out_set[3])
```

```python
import functools
import math

import jax
import jax.numpy as jnp
from jax import lax
from jax.experimental import pallas as pl
from jax.experimental.pallas import tpu as pltpu
from jax.sharding import PartitionSpec as P

HEADS = 12
HEAD_DIM = 64
FF = 3072


EPSILON = 1e-05
MOMENT = 0.9
KEEP_MEAN = 0.75
MASKED = -1e30

BF16 = jnp.bfloat16
F32 = jnp.float32
NN = (((1,), (0,)), ((), ()))
NT = (((1,), (1,)), ((), ()))
TN = (((0,), (0,)), ((), ()))


def mm(left, right, dims=NN):
    return lax.dot_general(left, right, dims, preferred_element_type=F32)


def swap(values, axis_name, bit):
    size = lax.axis_size(axis_name)
    return lax.ppermute(values, axis_name, [(i, i ^ bit) for i in range(size)])


def bits_of(axis_name):
    return [1 << i for i in range(lax.axis_size(axis_name).bit_length() - 1)]


def gather_bit(values, axis_name, bit, dim):
    other = swap(values, axis_name, bit)
    high = (lax.axis_index(axis_name) & bit) != 0
    return jnp.where(
        high, jnp.stack([other, values], axis=dim), jnp.stack([values, other], axis=dim)
    )


def gather_rows(block):
    rows, width = block.shape
    expert_bits, hidden_bits = bits_of("expert"), bits_of("hidden")
    for bit in expert_bits[1:]:
        block = gather_bit(block, "expert", bit, 0)
    block = block.reshape(-1, rows, width)
    outer = block.shape[0]
    half = width // 2 // 128 * 128
    up = block[:, :, :half]
    for bit in hidden_bits:
        up = gather_bit(up, "hidden", bit, 1)
    up = up.reshape(outer, -1, rows, half)
    down = block[:, :, half:]
    for step, bit in enumerate(reversed(hidden_bits)):
        down = gather_bit(down, "hidden", bit, 1 + step)
    down = down.reshape(outer, -1, rows, width - half)
    block = jnp.concatenate([up, down], axis=3)
    block = gather_bit(block, "expert", expert_bits[0], 1)
    return block.reshape(-1, width)


def pick(values, index, dim):
    return lax.dynamic_index_in_dim(values, index, dim, keepdims=False)


def reduce_bit(values, axis_name, bit, dim):
    mine = (lax.axis_index(axis_name) & bit) // bit
    other = swap(pick(values, 1 - mine, dim).astype(BF16), axis_name, bit)
    return pick(values, mine, dim) + other.astype(F32)


def reduce_rows(part, rows):
    width = part.shape[1]
    expert_bits, hidden_bits = bits_of("expert"), bits_of("hidden")
    n_outer = 1 << (len(expert_bits) - 1)
    part = part.reshape(n_outer, 2, -1, width)
    part = reduce_bit(part, "expert", expert_bits[0], 1)
    half = width // 2 // 128 * 128
    up = part[:, :, :half]
    for bit in reversed(hidden_bits):
        up = reduce_bit(up.reshape(n_outer, 2, -1, half), "hidden", bit, 1)
    down = part[:, :, half:]
    for step, bit in enumerate(hidden_bits):
        lead = 1 << (len(hidden_bits) - 1 - step)
        down = reduce_bit(
            down.reshape(n_outer, lead, 2, -1, width - half), "hidden", bit, 2
        )
    part = jnp.concatenate(
        [up.reshape(n_outer, rows, half), down.reshape(n_outer, rows, width - half)], axis=2
    )
    for bit in reversed(expert_bits[1:]):
        part = reduce_bit(part.reshape(2, -1, rows, width), "expert", bit, 0)
    return part.reshape(rows, width)


def spread_hidden(rows_own):
    half = rows_own.shape[0] // 2
    hidden_bits = bits_of("hidden")
    up, down = rows_own[:half], rows_own[half:]
    for bit in hidden_bits:
        up = jnp.concatenate([up, swap(up, "hidden", bit)], axis=0)
    for bit in reversed(hidden_bits):
        down = jnp.concatenate([down, swap(down, "hidden", bit)], axis=0)
    return jnp.concatenate([up, down], axis=0)


def collect_hidden(part_rows):
    half = part_rows.shape[0] // 2
    hidden_bits = bits_of("hidden")
    up, down = part_rows[:half], part_rows[half:]
    for bit in reversed(hidden_bits):
        size = up.shape[0] // 2
        up = up[:size].astype(F32) + swap(up[size:], "hidden", bit).astype(F32)
        up = up.astype(BF16)
    for bit in hidden_bits:
        size = down.shape[0] // 2
        down = down[:size].astype(F32) + swap(down[size:], "hidden", bit).astype(F32)
        down = down.astype(BF16)
    return jnp.concatenate([up, down], axis=0)


def to_experts(slots):
    return lax.all_to_all(slots, "expert", split_axis=0, concat_axis=0, tiled=True)


def head_parts(values, first_lane):
    lane = lax.broadcasted_iota(jnp.int32, values.shape, 1)
    return jnp.where(lane // HEAD_DIM == first_lane, values, 0.0)


def spare_lane(shape, head):
    lane = lax.broadcasted_iota(jnp.int32, shape, 1)
    return lane == (HEAD_DIM if head == 0 else 0)


def masked_keys(keys, head, length):
    key_pos = lax.broadcasted_iota(jnp.int32, keys.shape, 0)
    bias = jnp.where(key_pos < length, 0.0, MASKED)
    return jnp.where(spare_lane(keys.shape, head), bias, head_parts(keys, head)).astype(BF16)


def masked_queries(queries, head):
    return jnp.where(
        spare_lane(queries.shape, head), 1.0, head_parts(queries, head)
    ).astype(BF16)


def attend_forward_kernel(block, length_ref, q_ref, k_ref, v_ref, o_ref, lse_ref):
    pair = pl.program_id(0)
    length = length_ref[0]
    seq_len = q_ref.shape[0]
    scale = HEAD_DIM**-0.5
    queries = q_ref[...].astype(F32) * scale
    keys = k_ref[...].astype(F32)
    values = v_ref[...].astype(F32)

    @pl.when(pair == 0)
    def _():
        lse_ref[...] = jnp.zeros_like(lse_ref)

    heads = [
        (
            masked_queries(queries, head),
            masked_keys(keys, head, length),
            head_parts(values, head).astype(BF16),
        )
        for head in range(2)
    ]
    lane = lax.broadcasted_iota(jnp.int32, (block, 128), 1)
    on_diag = lax.broadcasted_iota(jnp.int32, (block, block), 0) >= lax.broadcasted_iota(
        jnp.int32, (block, block), 1
    )
    for index in range(seq_len // block):
        low, high = index * block, (index + 1) * block
        total = jnp.zeros((block, 128), F32)
        stats = lse_ref[low:high]
        for head in range(2):
            q_head, k_head, v_head = heads[head]
            diag = jnp.where(on_diag, mm(q_head[low:high], k_head[low:high], NT), MASKED)
            peak = jnp.max(diag, axis=1, keepdims=True)
            if index:
                past = mm(q_head[low:high], k_head[:low], NT)
                peak = jnp.maximum(peak, jnp.max(past, axis=1, keepdims=True))
            diag = jnp.exp(diag - peak)
            row_sum = jnp.sum(diag, axis=1, keepdims=True)
            mixed = mm(diag.astype(BF16), v_head[low:high])
            if index:
                past = jnp.exp(past - peak)
                row_sum = row_sum + jnp.sum(past, axis=1, keepdims=True)
                mixed = mixed + mm(past.astype(BF16), v_head[:low])
            total = total + mixed / row_sum
            stats = jnp.where(lane == 2 * pair + head, peak + jnp.log(row_sum), stats)
        o_ref[low:high] = total.astype(BF16)
        lse_ref[low:high] = stats


def attend_forward(qkv_rows, length, block):
    tok, width = qkv_rows.shape
    pairs = width // 3 // 128
    column = lambda offset: pl.BlockSpec((tok, 128), lambda i: (0, i + offset))
    return pl.pallas_call(
        functools.partial(attend_forward_kernel, block),
        grid=(pairs,),
        in_specs=[
            pl.BlockSpec(memory_space=pltpu.SMEM),
            column(0),
            column(pairs),
            column(2 * pairs),
        ],
        out_specs=[column(0), pl.BlockSpec((tok, 128), lambda i: (0, 0))],
        out_shape=[
            jax.ShapeDtypeStruct((tok, pairs * 128), BF16),
            jax.ShapeDtypeStruct((tok, 128), F32),
        ],
        name="attend_forward",
    )(length, qkv_rows, qkv_rows, qkv_rows)


def attend_backward_kernel(
    block, length_ref, q_ref, k_ref, v_ref, g_ref, lse_ref, dot_ref, dq_ref, dk_ref, dv_ref,
    dk_acc, dv_acc
):
    length = length_ref[0]
    seq_len = q_ref.shape[0]
    scale = HEAD_DIM**-0.5
    queries = q_ref[...].astype(F32) * scale
    keys = k_ref[...].astype(F32)
    grads = g_ref[...].astype(F32)
    values = v_ref[...]
    heads = [
        (
            masked_queries(queries, head),
            masked_keys(keys, head, length),
            head_parts(queries, head).astype(BF16),
            head_parts(keys * scale, head).astype(BF16),
            head_parts(grads, head).astype(BF16),
        )
        for head in range(2)
    ]
    on_diag = lax.broadcasted_iota(jnp.int32, (block, block), 0) <= lax.broadcasted_iota(
        jnp.int32, (block, block), 1
    )
    dk_acc[...] = jnp.zeros_like(dk_acc)
    dv_acc[...] = jnp.zeros_like(dv_acc)
    for index in range(seq_len // block):
        low, high = index * block, (index + 1) * block
        grad_q = jnp.zeros((block, 128), F32)
        for head in range(2):
            q_aug, k_aug, q_head, k_head, g_head = heads[head]
            lse = lse_ref[0, head : head + 1, low:high]
            row_dot = dot_ref[0, head : head + 1, low:high]
            for start, stop in ((0, low), (low, high)):
                if start == stop:
                    continue
                scores = mm(k_aug[start:stop], q_aug[low:high], NT)
                probs = jnp.exp(scores - lse)
                if start == low:
                    probs = jnp.where(on_diag, probs, 0.0)
                grad_p = mm(values[start:stop], g_head[low:high], NT)
                grad_s = (probs * (grad_p - row_dot)).astype(BF16)
                dv_acc[start:stop] += mm(probs.astype(BF16), g_head[low:high])
                dk_acc[start:stop] += mm(grad_s, q_head[low:high])
                grad_q = grad_q + mm(grad_s, k_head[start:stop], TN)
        dq_ref[low:high] = grad_q.astype(BF16)
    dk_ref[...] = dk_acc[...].astype(BF16)
    dv_ref[...] = dv_acc[...].astype(BF16)


def attend_backward(qkv_rows, grad_mixed, lse, row_dot, length, block):
    tok, width = qkv_rows.shape
    pairs = width // 3 // 128
    column = lambda offset: pl.BlockSpec((tok, 128), lambda i: (0, i + offset))
    row = pl.BlockSpec((1, 2, tok), lambda i: (i, 0, 0))
    return pl.pallas_call(
        functools.partial(attend_backward_kernel, block),
        grid=(pairs,),
        in_specs=[
            pl.BlockSpec(memory_space=pltpu.SMEM),
            column(0),
            column(pairs),
            column(2 * pairs),
            column(0),
            row,
            row,
        ],
        out_specs=[column(0)] * 3,
        out_shape=[jax.ShapeDtypeStruct((tok, pairs * 128), BF16)] * 3,
        scratch_shapes=[pltpu.VMEM((tok, 128), F32)] * 2,
        name="attend_backward",
    )(length, qkv_rows, qkv_rows, qkv_rows, grad_mixed, lse, row_dot)


def layer_norm(values, gain_row, shift_row):
    row_mean = jnp.mean(values, axis=-1, keepdims=True)
    centered = values - row_mean
    inverse = lax.rsqrt(jnp.mean(centered * centered, axis=-1, keepdims=True) + EPSILON)
    normed = centered * inverse
    return (normed * gain_row + shift_row, normed, inverse)


def norm_back(grad_rows, normed, inverse, gain_row):
    scaled = grad_rows * gain_row
    first_mean = jnp.mean(scaled, axis=-1, keepdims=True)
    second_mean = jnp.mean(scaled * normed, axis=-1, keepdims=True)
    grad_in = inverse * (scaled - first_mean - normed * second_mean)
    return (grad_in, jnp.sum(grad_rows * normed, axis=0), jnp.sum(grad_rows, axis=0))


def nesterov(master, momentum, average, grad_full, rate):
    moment_new = MOMENT * momentum + grad_full
    weight_new = master - rate * (grad_full + MOMENT * moment_new)
    return (grad_full, moment_new, weight_new, KEEP_MEAN * average + (1.0 - KEEP_MEAN) * weight_new)


def per_device(
    inputs,
    out_grad,
    seq_lengths,
    routes,
    norm_master,
    norm_momentum,
    norm_average,
    qkv_master,
    qkv_momentum,
    qkv_average,
    proj_master,
    proj_momentum,
    proj_average,
    router_master,
    router_momentum,
    router_average,
    frozen_in,
    frozen_out,
    expert_in_master,
    expert_in_momentum,
    expert_in_average,
    expert_out_master,
    expert_out_momentum,
    expert_out_average,
):
    tok_dev, model_width = inputs.shape
    seq_dev = seq_lengths.shape[0]
    assert seq_dev == 1
    n_expert = lax.axis_size("expert")
    n_hidden = lax.axis_size("hidden")
    experts = 2 * n_expert
    capacity = tok_dev * 2 // experts // 2
    slot_count = experts * capacity
    tokens_all = tok_dev * n_expert * n_hidden
    own_rows = model_width // (n_expert * n_hidden)
    block_rows = min(256, tok_dev)
    expert_index = lax.axis_index("expert")

    pad_norm = 128 - 4
    first_block = jnp.concatenate(
        [qkv_master, norm_master.T, jnp.zeros((own_rows, pad_norm), F32)], axis=1
    ).astype(BF16)
    pad_router = 128 - experts
    second_block = jnp.concatenate(
        [proj_master.T, router_master, jnp.zeros((own_rows, pad_router), F32)], axis=1
    ).astype(BF16)
    first_full = gather_rows(first_block)
    qkv_full = first_full[:, : 3 * model_width]
    norm_full = first_full[:, 3 * model_width :].astype(F32).T
    second_full = gather_rows(second_block)
    proj_full = second_full[:, :model_width]
    router_full = second_full[:, model_width:]

    row_ids = jnp.arange(tok_dev, dtype=jnp.int32)
    live_rows = row_ids < seq_lengths[0]
    live_float = live_rows.astype(F32)[:, None]
    expert_ids = jnp.arange(128, dtype=jnp.int32)
    match = [routes[:, k : k + 1] == expert_ids[None, :] for k in range(2)]
    counts = ((match[0] | match[1]) & live_rows[:, None]).astype(BF16)
    earlier = (row_ids[:, None] > row_ids[None, :]).astype(BF16)
    before = mm(earlier, counts)
    slot_ids = jnp.arange(slot_count, dtype=jnp.int32)
    chosen = None
    for k in range(2):
        rank = jnp.sum(jnp.where(match[k], before, 0.0), axis=1).astype(jnp.int32)
        kept = live_rows & (rank < capacity)
        expert_of = routes[:, k]
        slot = (expert_of % 2 * n_expert + expert_of // 2) * capacity + rank
        hit = jnp.where(kept, slot, -1)[:, None] == slot_ids[None, :]
        chosen = hit if chosen is None else chosen | hit
    select = chosen.astype(BF16)

    route_part = jnp.concatenate(
        [routes.astype(BF16), jnp.zeros((tok_dev, 126), BF16)], axis=1
    )
    grad_out_rows = jnp.where(live_rows[:, None], out_grad, jnp.zeros_like(out_grad))
    early = jnp.concatenate([grad_out_rows, route_part], axis=1)
    early_slots = mm(select, early, TN).astype(BF16)
    early_slots = early_slots.reshape(2, n_expert, capacity, model_width + 128)
    weight_in = (frozen_in[0], expert_in_master[0].astype(BF16))
    weight_out = (frozen_out[0], expert_out_master[0].astype(BF16))
    grad_rows, back_hidden = [], []
    for part in range(2):
        group = spread_hidden(to_experts(early_slots[part]).reshape(-1, model_width + 128))
        grad_rows.append(group)
        back_hidden.append(mm(group[:, :model_width], weight_out[part], NT))

    resid_in = inputs.astype(F32)
    normed_one, base_one, inverse_one = layer_norm(resid_in, norm_full[0], norm_full[1])
    attn_in = normed_one.astype(BF16)
    qkv_rows = mm(attn_in, qkv_full).astype(BF16)
    attn_out, log_totals = attend_forward(qkv_rows, seq_lengths, block_rows)
    resid_mid = resid_in + mm(attn_out, proj_full, NT)
    normed_two, base_two, inverse_two = layer_norm(resid_mid, norm_full[2], norm_full[3])
    moe_in = normed_two.astype(BF16)

    moe_slots = mm(select, moe_in, TN).astype(BF16).reshape(2, n_expert, capacity, model_width)
    returned, value_parts, router_part = [], [], 0.0
    weight_grads = None
    for part in range(2):
        rows = spread_hidden(to_experts(moe_slots[part]).reshape(-1, model_width))
        group = grad_rows[part]
        own = 2 * expert_index + part
        route_sum = group[:, model_width].astype(F32) + group[:, model_width + 1].astype(F32)
        other = route_sum.astype(jnp.int32) - own
        is_own = (expert_ids == own).astype(F32)[None, :]
        signs = is_own - (other[:, None] == expert_ids[None, :]).astype(F32)
        gap = jnp.sum(mm(rows, router_full) * signs, axis=1, keepdims=True)
        gate = jax.nn.sigmoid(gap)
        pre_act = mm(rows, weight_in[part])
        root = math.sqrt(2.0 / math.pi)
        squared = pre_act * pre_act
        curve = jnp.tanh(root * pre_act * (1.0 + 0.044715 * squared))
        activation = (0.5 * pre_act * (1.0 + curve)).astype(BF16)
        slope = 0.5 * (1.0 + curve) + 0.5 * pre_act * (1.0 - curve * curve) * root * (
            1.0 + 3 * 0.044715 * squared
        )
        back = back_hidden[part]
        grad_pre = (slope * (gate * back)).astype(BF16)
        grad_gate = jnp.sum(activation.astype(F32) * back, axis=1, keepdims=True)
        grad_logit = (gate * (1.0 - gate) * grad_gate * signs).astype(BF16)
        grad_in = (mm(grad_pre, weight_in[part], NT) + mm(grad_logit, router_full, NT)).astype(BF16)
        returned.append(to_experts(collect_hidden(grad_in).reshape(n_expert, capacity, model_width)))
        value_parts.append((gate * mm(activation, weight_out[part])).astype(BF16))
        router_part = router_part + mm(rows, grad_logit, TN)
        if part == 1:
            pair_grad = (gate * group[:, :model_width].astype(F32)).astype(BF16)
            weight_grads = (mm(rows, grad_pre, TN), mm(activation, pair_grad, TN))

    back_slots = jnp.concatenate(returned, axis=0).reshape(slot_count, model_width)
    grad_norm_two = mm(select, back_slots)
    grad_out = grad_out_rows.astype(F32)
    grad_low_two, gain_two_grad, shift_two_grad = norm_back(
        grad_norm_two, base_two, inverse_two, norm_full[2]
    )
    grad_mid = grad_out + grad_low_two
    grad_branch = grad_mid.astype(BF16)
    grad_attn = mm(grad_branch, proj_full).astype(BF16)

    value_slots = jnp.concatenate(
        [
            to_experts(collect_hidden(rows).reshape(n_expert, capacity, model_width))
            for rows in value_parts
        ],
        axis=0,
    ).reshape(slot_count, model_width)
    outputs = (live_float * (resid_mid + mm(select, value_slots))).astype(BF16)

    head_of = jnp.arange(model_width, dtype=jnp.int32) // HEAD_DIM
    head_sums = (head_of[None, :] == jnp.arange(HEADS, dtype=jnp.int32)[:, None]).astype(F32)
    row_dot = lax.dot_general(
        head_sums,
        grad_attn.astype(F32) * attn_out.astype(F32),
        NT,
        precision=lax.Precision.HIGHEST,
        preferred_element_type=F32,
    ).reshape(HEADS // 2, 2, tok_dev)
    log_rows = log_totals.T[:HEADS].reshape(HEADS // 2, 2, tok_dev)
    grad_q, grad_k, grad_v = attend_backward(
        qkv_rows, grad_attn, log_rows, row_dot, seq_lengths, block_rows
    )
    grad_qkv = jnp.concatenate([grad_q, grad_k, grad_v], axis=1)
    qkv_part = mm(attn_in, grad_qkv, TN)
    grad_norm_one = mm(grad_qkv, qkv_full, NT)
    grad_low_one, gain_one_grad, shift_one_grad = norm_back(
        grad_norm_one, base_one, inverse_one, norm_full[0]
    )
    input_grad = grad_mid + grad_low_one

    proj_part = mm(grad_branch, attn_out, TN)
    early_sums = reduce_rows(jnp.concatenate([proj_part, router_part], axis=1), own_rows)
    proj_sum = early_sums[:, :model_width].T
    router_sum = early_sums[:, model_width : model_width + experts]
    norm_part = jnp.stack([gain_one_grad, shift_one_grad, gain_two_grad, shift_two_grad], axis=1)
    norm_part = jnp.concatenate([norm_part, jnp.zeros((model_width, 124), F32)], axis=1)
    late_sums = reduce_rows(jnp.concatenate([qkv_part, norm_part], axis=1), own_rows)
    qkv_sum = late_sums[:, : 3 * model_width]
    norm_sum = late_sums[:, 3 * model_width : 3 * model_width + 4].T

    norm_rate = 0.1 / math.sqrt(tokens_all)
    qkv_rate = 1.0 / math.sqrt(model_width * tokens_all)
    proj_rate = 40.0 / math.sqrt(model_width * tokens_all)
    router_rate = 0.08 * math.sqrt(experts / (model_width * tokens_all))
    in_rate = 5.0 * math.sqrt(experts / (model_width * tokens_all))
    out_rate = 2.5 * math.sqrt(experts / (FF * tokens_all))
    norm_set = nesterov(norm_master, norm_momentum, norm_average, norm_sum, norm_rate)
    qkv_set = nesterov(qkv_master, qkv_momentum, qkv_average, qkv_sum, qkv_rate)
    proj_set = nesterov(proj_master, proj_momentum, proj_average, proj_sum, proj_rate)
    router_set = nesterov(router_master, router_momentum, router_average, router_sum, router_rate)
    in_set = nesterov(
        expert_in_master, expert_in_momentum, expert_in_average, weight_grads[0][None], in_rate
    )
    out_set = nesterov(
        expert_out_master, expert_out_momentum, expert_out_average, weight_grads[1][None], out_rate
    )
    return (
        outputs,
        input_grad,
        *norm_set,
        *qkv_set,
        *proj_set,
        *router_set,
        *in_set,
        *out_set,
    )


def solution(mesh):
    rows = P(("expert", "hidden"), None)
    columns = P(None, ("expert", "hidden"))
    expert_in = P("expert", None, "hidden")
    expert_out = P("expert", "hidden", None)
    return jax.shard_map(
        per_device,
        mesh=mesh,
        in_specs=(
            rows,
            rows,
            P(("expert", "hidden")),
            rows,
            *[columns] * 3,
            *[rows] * 3,
            *[columns] * 3,
            *[rows] * 3,
            expert_in,
            expert_out,
            *[expert_in] * 3,
            *[expert_out] * 3,
        ),
        out_specs=(
            rows,
            rows,
            *[columns] * 4,
            *[rows] * 4,
            *[columns] * 4,
            *[rows] * 4,
            *[expert_in] * 4,
            *[expert_out] * 4,
        ),
        check_vma=False,
    )
```

```python
import functools
import math

import jax
import jax.numpy as jnp
from jax import lax
from jax.experimental import pallas as pl
from jax.experimental.pallas import tpu as pltpu
from jax.sharding import PartitionSpec as P

HEADS = 12
HEAD_DIM = 64
FF = 3072


EPSILON = 1e-05
MOMENT = 0.9
KEEP_MEAN = 0.75
MASKED = -1e30
HEAD_ROWS = 16

BF16 = jnp.bfloat16
F32 = jnp.float32
NN = (((1,), (0,)), ((), ()))
NT = (((1,), (1,)), ((), ()))
TN = (((0,), (0,)), ((), ()))


def mm(left, right, dims=NN):
    return lax.dot_general(left, right, dims, preferred_element_type=F32)


def cost(micros):
    return pl.CostEstimate(flops=int(micros * 1e6), transcendentals=0, bytes_accessed=1 << 20)


def together(*values):
    return lax.optimization_barrier(values)


def after(value, *earlier):
    return lax.optimization_barrier((value, *earlier))[0]


def swap(values, axis_name, bits):
    size = lax.axis_size(axis_name)
    return lax.ppermute(values, axis_name, [(i, i ^ bits) for i in range(size)])


def bits_of(axis_name):
    return [1 << i for i in range(lax.axis_size(axis_name).bit_length() - 1)]


def device_number():
    return lax.axis_index("expert") * lax.axis_size("hidden") + lax.axis_index("hidden")


def to_experts(slots, dim=0):
    return lax.all_to_all(slots, "expert", split_axis=dim, concat_axis=dim, tiled=True)


def gather_far(block):
    far = [swap(block, "expert", 2 * k) for k in range(1, lax.axis_size("expert") // 2)]
    return jnp.stack([block, *far])


def gather_near(blocks, split):
    n_hidden = lax.axis_size("hidden")
    hidden_bits = bits_of("hidden")
    pieces = []
    for low, high, order in (
        (0, split, hidden_bits),
        (split, blocks.shape[2], hidden_bits[::-1]),
    ):
        part = blocks[:, :, low:high]
        places = [2 * k * n_hidden for k in range(part.shape[0])]
        for bit in order:
            part = jnp.concatenate([part, swap(part, "hidden", bit)], axis=0)
            places = places + [p ^ bit for p in places]
        pieces.append((part, places, low))
    return pieces


def gather_core(pieces):
    n_hidden = lax.axis_size("hidden")
    return pieces + [
        (swap(part, "expert", 1), [p ^ n_hidden for p in places], low)
        for part, places, low in pieces
    ]


def aligned(rows):
    return rows % 8 == 0


def as_operands(pieces):
    rows = pieces[0][0].shape[1]
    if aligned(rows):
        plan = [
            (index, row, place, low, part.shape[2])
            for index, (part, places, low) in enumerate(pieces)
            for row, place in enumerate(places)
        ]
        return [part for part, _, _ in pieces], plan
    columns = []
    for low in sorted({low for _, _, low in pieces}):
        some = [piece for piece in pieces if piece[2] == low]
        places = [p for _, places, _ in some for p in places]
        order = sorted(range(len(places)), key=lambda i: places[i])
        stacked = jnp.concatenate([part for part, _, _ in some], axis=0)[jnp.array(order)]
        columns.append(stacked)
    whole = jnp.concatenate(columns, axis=2)
    whole = whole[device_number() ^ jnp.arange(whole.shape[0])]
    return [whole.reshape(-1, whole.shape[2])], None


def place_pieces(plan, me, piece_refs, whole_ref, sems):
    if plan is None:
        return [pltpu.make_async_copy(piece_refs[0], whole_ref, sems.at[0])]
    rows = piece_refs[0].shape[1]
    copies = []
    for number, (index, row, place, low, width) in enumerate(plan):
        start = pl.multiple_of((me ^ place) * rows, 8)
        copies.append(
            pltpu.make_async_copy(
                piece_refs[index].at[row],
                whole_ref.at[pl.ds(start, rows), pl.ds(low, width)],
                sems.at[number],
            )
        )
    return copies


def sum_orders():
    n_hidden = lax.axis_size("hidden")
    n_far = lax.axis_size("expert") // 2
    hidden_bits = bits_of("hidden")
    orders = []
    for bits in (hidden_bits[::-1], hidden_bits):
        places = [2 * k * n_hidden for k in range(n_far)]
        for bit in bits[::-1]:
            places = places + [p ^ bit for p in places]
        orders.append(places + [p ^ n_hidden for p in places])
    return orders


def bundle(weight_in, weight_out):
    if weight_in.shape == weight_out.shape:
        return [jnp.stack([weight_in, weight_out])]
    return [weight_in[None], weight_out[None]]


def reduce_steps(kept, sent, split):
    hidden_bits = bits_of("hidden")
    n_far = lax.axis_size("expert") // 2
    (arrived,) = yield [swap(sent, "expert", 1)]
    total = kept + arrived.astype(F32)
    up, down = total[:, :split], total[:, split:]
    for up_bit, down_bit in zip(hidden_bits[::-1], hidden_bits):
        half = up.shape[0] // 2
        up_arrived, down_arrived = yield [
            swap(up[half:].astype(BF16), "hidden", up_bit),
            swap(down[half:].astype(BF16), "hidden", down_bit),
        ]
        up = up[:half] + up_arrived.astype(F32)
        down = down[:half] + down_arrived.astype(F32)
    total = jnp.concatenate([up, down], axis=1)
    rows = total.shape[0] // n_far
    away = total.astype(BF16)
    arrived = yield [
        swap(away[k * rows : (k + 1) * rows], "expert", 2 * k) for k in range(1, n_far)
    ]
    yield total[:rows] + sum(part.astype(F32) for part in arrived)


def behind(steps, arrived, *earlier):
    tied = together(*arrived, *earlier)
    return steps.send(tied[: len(arrived)]), tied[len(arrived) :]


def finish(steps, arrived):
    while isinstance(arrived, list):
        arrived = steps.send(arrived)
    return arrived


def spread(rows, bits):
    near = rows[None]
    for bit in bits[:-1]:
        near = jnp.concatenate([near, swap(near, "hidden", bit)], axis=0)
    return near, swap(near, "hidden", bits[-1])


def collect(near, far, bits):
    total = near + far.astype(F32)
    for bit in bits[-2::-1]:
        half = total.shape[0] // 2
        total = total[:half] + swap(total[half:].astype(BF16), "hidden", bit).astype(F32)
    return total.astype(BF16)


def head_parts(values, first_lane):
    lane = lax.broadcasted_iota(jnp.int32, values.shape, 1)
    return jnp.where(lane // HEAD_DIM == first_lane, values, 0.0)


def spare_lane(shape, head):
    lane = lax.broadcasted_iota(jnp.int32, shape, 1)
    return lane == (HEAD_DIM if head == 0 else 0)


def masked_keys(keys, head, length):
    key_pos = lax.broadcasted_iota(jnp.int32, keys.shape, 0)
    bias = jnp.where(key_pos < length, 0.0, MASKED)
    return jnp.where(spare_lane(keys.shape, head), bias, head_parts(keys, head)).astype(BF16)


def masked_queries(queries, head):
    return jnp.where(
        spare_lane(queries.shape, head), 1.0, head_parts(queries, head)
    ).astype(BF16)


def attend_forward_kernel(block, length_ref, q_ref, k_ref, v_ref, o_ref, rows_ref, lse_ref):
    pair = pl.program_id(0)
    length = length_ref[0]
    seq_len = q_ref.shape[0]
    scale = HEAD_DIM**-0.5
    queries = q_ref[...].astype(F32) * scale
    keys = k_ref[...].astype(F32)
    values = v_ref[...].astype(F32)

    @pl.when(pair == 0)
    def _():
        lse_ref[...] = jnp.zeros_like(lse_ref)

    heads = [
        (
            masked_queries(queries, head),
            masked_keys(keys, head, length),
            head_parts(values, head).astype(BF16),
        )
        for head in range(2)
    ]
    lane = lax.broadcasted_iota(jnp.int32, (block, 128), 1)
    on_diag = lax.broadcasted_iota(jnp.int32, (block, block), 0) >= lax.broadcasted_iota(
        jnp.int32, (block, block), 1
    )
    for index in range(seq_len // block):
        low, high = index * block, (index + 1) * block
        total = jnp.zeros((block, 128), F32)
        stats = lse_ref[low:high]
        for head in range(2):
            q_head, k_head, v_head = heads[head]
            diag = jnp.where(on_diag, mm(q_head[low:high], k_head[low:high], NT), MASKED)
            peak = jnp.max(diag, axis=1, keepdims=True)
            if index:
                past = mm(q_head[low:high], k_head[:low], NT)
                peak = jnp.maximum(peak, jnp.max(past, axis=1, keepdims=True))
            diag = jnp.exp(diag - peak)
            row_sum = jnp.sum(diag, axis=1, keepdims=True)
            mixed = mm(diag.astype(BF16), v_head[low:high])
            if index:
                past = jnp.exp(past - peak)
                row_sum = row_sum + jnp.sum(past, axis=1, keepdims=True)
                mixed = mixed + mm(past.astype(BF16), v_head[:low])
            total = total + mixed / row_sum
            stats = jnp.where(lane == 2 * pair + head, peak + jnp.log(row_sum), stats)
        o_ref[low:high] = total.astype(BF16)
        lse_ref[low:high] = stats

    @pl.when(pair == pl.num_programs(0) - 1)
    def _():
        rows_ref[...] = lse_ref[...].T[: rows_ref.shape[0]]


def attend_forward(qkv_rows, length, block):
    tok, width = qkv_rows.shape
    pairs = width // 3 // 128
    column = lambda offset: pl.BlockSpec((tok, 128), lambda i: (0, i + offset))
    return pl.pallas_call(
        functools.partial(attend_forward_kernel, block),
        grid=(pairs,),
        in_specs=[
            pl.BlockSpec(memory_space=pltpu.SMEM),
            column(0),
            column(pairs),
            column(2 * pairs),
        ],
        out_specs=[column(0), pl.BlockSpec((HEAD_ROWS, tok), lambda i: (0, 0))],
        out_shape=[
            jax.ShapeDtypeStruct((tok, pairs * 128), BF16),
            jax.ShapeDtypeStruct((HEAD_ROWS, tok), F32),
        ],
        scratch_shapes=[pltpu.VMEM((tok, 128), F32)],
        cost_estimate=cost(23),
        name="attend_forward",
    )(length, qkv_rows, qkv_rows, qkv_rows)


def attend_backward_kernel(
    block, first, length_ref, q_ref, k_ref, v_ref, g_ref, lse_ref, dot_ref, dq_ref, dk_ref, dv_ref,
    dk_acc, dv_acc
):
    length = length_ref[0]
    seq_len = q_ref.shape[0]
    scale = HEAD_DIM**-0.5
    queries = q_ref[...].astype(F32) * scale
    keys = k_ref[...].astype(F32)
    grads = g_ref[...].astype(F32)
    values = v_ref[...]
    heads = [
        (
            masked_queries(queries, head),
            masked_keys(keys, head, length),
            head_parts(queries, head).astype(BF16),
            head_parts(keys * scale, head).astype(BF16),
            head_parts(grads, head).astype(BF16),
        )
        for head in range(2)
    ]
    on_diag = lax.broadcasted_iota(jnp.int32, (block, block), 0) <= lax.broadcasted_iota(
        jnp.int32, (block, block), 1
    )
    dk_acc[...] = jnp.zeros_like(dk_acc)
    dv_acc[...] = jnp.zeros_like(dv_acc)
    for index in range(seq_len // block):
        low, high = index * block, (index + 1) * block
        grad_q = jnp.zeros((block, 128), F32)
        for head in range(2):
            q_aug, k_aug, q_head, k_head, g_head = heads[head]
            row = 2 * (first + pl.program_id(0)) + head
            lse = lse_ref[pl.ds(row, 1), low:high]
            row_dot = dot_ref[pl.ds(row, 1), low:high]
            for start, stop in ((0, low), (low, high)):
                if start == stop:
                    continue
                scores = mm(k_aug[start:stop], q_aug[low:high], NT)
                probs = jnp.exp(scores - lse)
                if start == low:
                    probs = jnp.where(on_diag, probs, 0.0)
                grad_p = mm(values[start:stop], g_head[low:high], NT)
                grad_s = (probs * (grad_p - row_dot)).astype(BF16)
                dv_acc[start:stop] += mm(probs.astype(BF16), g_head[low:high])
                dk_acc[start:stop] += mm(grad_s, q_head[low:high])
                grad_q = grad_q + mm(grad_s, k_head[start:stop], TN)
        dq_ref[low:high] = grad_q.astype(BF16)
    dk_ref[...] = dk_acc[...].astype(BF16)
    dv_ref[...] = dv_acc[...].astype(BF16)


def attend_backward(qkv_rows, grad_mixed, lse, row_dot, length, block, first, count):
    tok, width = qkv_rows.shape
    pairs = width // 3 // 128
    column = lambda offset: pl.BlockSpec((tok, 128), lambda i: (0, i + offset))
    whole = pl.BlockSpec((HEAD_ROWS, tok), lambda i: (0, 0))
    return pl.pallas_call(
        functools.partial(attend_backward_kernel, block, first),
        grid=(count,),
        in_specs=[
            pl.BlockSpec(memory_space=pltpu.SMEM),
            column(first),
            column(pairs + first),
            column(2 * pairs + first),
            column(first),
            whole,
            whole,
        ],
        out_specs=[column(0)] * 3,
        out_shape=[jax.ShapeDtypeStruct((tok, count * 128), BF16)] * 3,
        scratch_shapes=[pltpu.VMEM((tok, 128), F32)] * 2,
        cost_estimate=cost(17),
        name="attend_backward",
    )(length, qkv_rows, qkv_rows, qkv_rows, grad_mixed, lse, row_dot)


def centre(values):
    row_mean = jnp.mean(values, axis=-1, keepdims=True)
    centered = values - row_mean
    inverse = lax.rsqrt(jnp.mean(centered * centered, axis=-1, keepdims=True) + EPSILON)
    return centered * inverse, inverse


def norm_back(grad_rows, normed, inverse, gain_row):
    scaled = grad_rows * gain_row
    first_mean = jnp.mean(scaled, axis=-1, keepdims=True)
    second_mean = jnp.mean(scaled * normed, axis=-1, keepdims=True)
    return inverse * (scaled - first_mean - normed * second_mean)


def column_sums(ref, normed, grad_rows):
    @pl.when(pl.program_id(0) == 0)
    def _():
        ref[...] = jnp.zeros_like(ref)

    ref[0:1] += jnp.sum(grad_rows * normed, axis=0, keepdims=True)
    ref[1:2] += jnp.sum(grad_rows, axis=0, keepdims=True)


def any_space(count):
    return [pl.BlockSpec(memory_space=pl.ANY)] * count


def row_block(block, width):
    return pl.BlockSpec((block, width), lambda i: (i, 0))


def fixed(*shape):
    return pl.BlockSpec(shape, lambda i: (0,) * len(shape))


def project_in_kernel(plan, count, width, norm_low, me_ref, x_ref, *refs):
    piece_refs, (qkv_ref, attn_in_ref, whole_ref, norm_ref, sems) = refs[:count], refs[count:]
    copies = place_pieces(plan, me_ref[0], piece_refs, whole_ref, sems)
    first = pl.program_id(0) == 0

    @pl.when(first)
    def _():
        for copy in copies:
            copy.start()

    normed, _ = centre(x_ref[...].astype(F32))

    @pl.when(first)
    def _():
        for copy in copies:
            copy.wait()
        row = lax.broadcasted_iota(jnp.int32, (8, 128), 0)
        lane = lax.broadcasted_iota(jnp.int32, (8, 128), 1)
        norm_ref[...] = mm((row == lane).astype(BF16), whole_ref[:, norm_low : norm_low + 128], NT)

    attn_in = (normed * norm_ref[0:1] + norm_ref[1:2]).astype(BF16)
    attn_in_ref[...] = attn_in
    qkv_ref[...] = mm(attn_in, whole_ref[:, :width]).astype(BF16)


def project_in(inputs, pieces, width, norm_low, whole_width, block):
    tok, model_width = inputs.shape
    operands, plan = as_operands(pieces)
    return pl.pallas_call(
        functools.partial(project_in_kernel, plan, len(operands), width, norm_low),
        grid=(tok // block,),
        in_specs=[
            pl.BlockSpec(memory_space=pltpu.SMEM),
            row_block(block, model_width),
            *any_space(len(operands)),
        ],
        out_specs=[
            row_block(block, width),
            row_block(block, model_width),
            fixed(model_width, whole_width),
            fixed(8, model_width),
        ],
        out_shape=[
            jax.ShapeDtypeStruct((tok, width), BF16),
            jax.ShapeDtypeStruct((tok, model_width), BF16),
            jax.ShapeDtypeStruct((model_width, whole_width), BF16),
            jax.ShapeDtypeStruct((8, model_width), F32),
        ],
        scratch_shapes=[pltpu.SemaphoreType.DMA((len(plan) if plan else 1,))],
        cost_estimate=cost(9),
        name="project_in",
    )(device_number()[None], inputs, *operands)


def project_out_kernel(x_ref, o_ref, norm_ref, weight_ref, resid_ref, moe_in_ref):
    resid = x_ref[...].astype(F32) + mm(o_ref[...], weight_ref[...], NT)
    resid_ref[...] = resid
    normed, _ = centre(resid)
    moe_in_ref[...] = (normed * norm_ref[2:3] + norm_ref[3:4]).astype(BF16)


def columns_of(array, low, width):
    assert low % width == 0
    return pl.BlockSpec((array.shape[0], width), lambda i: (0, low // width))


def project_out(inputs, attn_out, norm_rows, weight, low, block):
    tok, width = inputs.shape
    return pl.pallas_call(
        project_out_kernel,
        grid=(tok // block,),
        in_specs=[
            row_block(block, width),
            row_block(block, width),
            fixed(8, width),
            columns_of(weight, low, width),
        ],
        out_specs=[row_block(block, width), row_block(block, width)],
        out_shape=[
            jax.ShapeDtypeStruct((tok, width), F32),
            jax.ShapeDtypeStruct((tok, width), BF16),
        ],
        cost_estimate=cost(7),
        name="project_out",
    )(inputs, attn_out, norm_rows, weight)


def middle_back_kernel(
    select_ref, first_ref, second_ref, resid_ref, grad_ref, o_ref, norm_ref, weight_ref,
    grad_mid_ref, branch_ref, grad_attn_ref, dot_ref, sums_ref
):
    width = resid_ref.shape[1]
    count = first_ref.shape[0]
    grad_rows = mm(select_ref[:, :count], first_ref[...])
    grad_rows = grad_rows + mm(select_ref[:, count:], second_ref[...])
    normed, inverse = centre(resid_ref[...])
    grad_mid = grad_ref[...].astype(F32) + norm_back(grad_rows, normed, inverse, norm_ref[2:3])
    column_sums(sums_ref, normed, grad_rows)
    grad_mid_ref[...] = grad_mid
    branch = grad_mid.astype(BF16)
    branch_ref[...] = branch
    grad_attn = mm(branch, weight_ref[...]).astype(BF16)
    grad_attn_ref[...] = grad_attn
    product = grad_attn.astype(F32) * o_ref[...].astype(F32)
    upper = product.astype(BF16)
    lower = (product - upper.astype(F32)).astype(BF16)
    head = lax.broadcasted_iota(jnp.int32, (HEAD_ROWS, width), 0)
    lane = lax.broadcasted_iota(jnp.int32, (HEAD_ROWS, width), 1)
    ones = (lane // HEAD_DIM == head).astype(BF16)
    dot_ref[...] = mm(ones, upper, NT) + mm(ones, lower, NT)


def middle_back(select, first, second, resid, grad_out, attn_out, norm_rows, weight, low, block):
    tok, width = resid.shape
    return pl.pallas_call(
        middle_back_kernel,
        grid=(tok // block,),
        in_specs=[
            row_block(block, select.shape[1]),
            fixed(*first.shape),
            fixed(*second.shape),
            row_block(block, width),
            row_block(block, width),
            row_block(block, width),
            fixed(8, width),
            columns_of(weight, low, width),
        ],
        out_specs=[
            row_block(block, width),
            row_block(block, width),
            row_block(block, width),
            pl.BlockSpec((HEAD_ROWS, block), lambda i: (0, i)),
            fixed(8, width),
        ],
        out_shape=[
            jax.ShapeDtypeStruct((tok, width), F32),
            jax.ShapeDtypeStruct((tok, width), BF16),
            jax.ShapeDtypeStruct((tok, width), BF16),
            jax.ShapeDtypeStruct((HEAD_ROWS, tok), F32),
            jax.ShapeDtypeStruct((8, width), F32),
        ],
        cost_estimate=cost(12),
        name="middle_back",
    )(select, first, second, resid, grad_out, attn_out, norm_rows, weight)


def last_back_kernel(
    spans, count, x_ref, grad_mid_ref, norm_ref, weight_ref, *refs
):
    grad_refs, (out_ref, sums_ref) = refs[:count], refs[count:]
    grad_rows = None
    for ref, low in zip(grad_refs, spans):
        term = mm(ref[...], weight_ref[:, low : low + ref.shape[1]], NT)
        grad_rows = term if grad_rows is None else grad_rows + term
    normed, inverse = centre(x_ref[...].astype(F32))
    out_ref[...] = grad_mid_ref[...] + norm_back(grad_rows, normed, inverse, norm_ref[0:1])
    column_sums(sums_ref, normed, grad_rows)


def last_back(inputs, grad_mid, norm_rows, weight, grads, spans, block):
    tok, width = inputs.shape
    return pl.pallas_call(
        functools.partial(last_back_kernel, spans, len(grads)),
        grid=(tok // block,),
        in_specs=[
            row_block(block, width),
            row_block(block, width),
            fixed(8, width),
            columns_of(weight, 0, 3 * width),
            *[row_block(block, grad.shape[1]) for grad in grads],
        ],
        out_specs=[row_block(block, width), fixed(8, width)],
        out_shape=[
            jax.ShapeDtypeStruct((tok, width), F32),
            jax.ShapeDtypeStruct((8, width), F32),
        ],
        cost_estimate=cost(11),
        name="last_back",
    )(inputs, grad_mid, norm_rows, weight, *grads)


def fill_sums(total_ref, pairs, extra_refs, row_refs):
    low = 0
    for left_ref, right_ref in pairs:
        high = low + right_ref.shape[1]
        total_ref[:, low:high] = mm(left_ref[...], right_ref[...], TN)
        low = high
    for ref in extra_refs:
        total_ref[:, low : low + ref.shape[1]] = ref[...]
        low += ref.shape[1]
    if row_refs:
        rows = [ref[...] for ref in row_refs]
        pad = 128 - sum(part.shape[0] for part in rows)
        rows.append(jnp.zeros((pad, rows[0].shape[1]), F32))
        total_ref[:, low : low + 128] = jnp.concatenate(rows, axis=0).T


def weight_sums_kernel(orders, rows, split, index, me_ref, *refs):
    lefts, rights, extras, row_parts, refs = (
        refs[: index[0]], refs[index[0] : index[1]], refs[index[1] : index[2]],
        refs[index[2] : index[3]], refs[index[3] :],
    )
    pairs = [(lefts[min(k, len(lefts) - 1)], right) for k, right in enumerate(rights)]
    if orders is None:
        fill_sums(refs[0], pairs, extras, row_parts)
        return
    keep, send, total_ref = refs
    fill_sums(total_ref, pairs, extras, row_parts)
    me = me_ref[0]
    for order, first, last in ((orders[0], 0, split), (orders[1], split, keep.shape[1])):
        half = len(order) // 2
        for place, relative in enumerate(order):
            start = pl.multiple_of((me ^ relative) * rows, 8)
            value = total_ref[pl.ds(start, rows), first:last]
            if place < half:
                keep[place * rows : (place + 1) * rows, first:last] = value
            else:
                low = (place - half) * rows
                send[low : low + rows, first:last] = value.astype(BF16)


def weight_sums(lefts, rights, extras, row_parts, split, rows):
    width = sum(array.shape[1] for array in (*rights, *extras)) + (128 if row_parts else 0)
    model_width = lefts[0].shape[1]
    orders = sum_orders()
    half = model_width // 2
    arrays = (*lefts, *rights, *extras, *row_parts)
    index = [len(lefts), len(lefts) + len(rights)]
    index += [index[1] + len(extras), len(arrays)]
    direct = aligned(rows)
    call = pl.pallas_call(
        functools.partial(weight_sums_kernel, orders if direct else None, rows, split, index),
        grid=(1,),
        in_specs=[
            pl.BlockSpec(memory_space=pltpu.SMEM),
            *[fixed(*array.shape) for array in arrays],
        ],
        out_specs=[fixed(half, width)] * 2 if direct else [fixed(model_width, width)],
        out_shape=(
            [jax.ShapeDtypeStruct((half, width), dtype) for dtype in (F32, BF16)]
            if direct
            else [jax.ShapeDtypeStruct((model_width, width), F32)]
        ),
        scratch_shapes=[pltpu.VMEM((model_width, width), F32)] if direct else [],
        cost_estimate=cost(6),
        name="weight_sums",
    )(device_number()[None], *arrays)
    if direct:
        return call
    blocks = call[0].reshape(-1, rows, width)
    ordered = [
        blocks[device_number() ^ jnp.array(order)].reshape(model_width, width)[:, columns]
        for order, columns in zip(orders, (slice(0, split), slice(split, width)))
    ]
    total = jnp.concatenate(ordered, axis=1)
    return total[:half], total[half:].astype(BF16)


def expert_kernel(
    me_ref, rows_ref, group_ref, router_ref, in_own, out_own, in_far, out_far,
    act_ref, grad_pre_ref, pair_ref, gate_ref, logit_ref, grad_ref,
    back_sum, total_ref
):
    step, steps = pl.program_id(0), pl.num_programs(0)
    width = rows_ref.shape[1]
    lane = lax.broadcasted_iota(jnp.int32, (rows_ref.shape[0], 128), 1)

    @pl.when(step == 0)
    def _():
        own = me_ref[0]
        route = group_ref[0, :, width:].astype(F32)
        other = (route[:, 0:1] + route[:, 1:2]).astype(jnp.int32) - own
        signs = (lane == own).astype(F32) - (lane == other).astype(F32)
        gap = jnp.sum(mm(rows_ref[...], router_ref[...]) * signs, axis=1, keepdims=True)
        gate = jax.nn.sigmoid(gap)
        gate_ref[...] = jnp.broadcast_to(gate, gate_ref.shape)
        logit_ref[...] = signs.astype(BF16)
        pair_ref[...] = (gate * group_ref[0, :, :width].astype(F32)).astype(BF16)
        back_sum[...] = jnp.zeros_like(back_sum)
        total_ref[...] = jnp.zeros_like(total_ref)

    def chunk(weight_in, weight_out):
        back = mm(group_ref[0, :, :width], weight_out, NT)
        pre_act = mm(rows_ref[...], weight_in)
        gate = gate_ref[:, 0:1]
        root = math.sqrt(2.0 / math.pi)
        squared = pre_act * pre_act
        curve = jnp.tanh(pre_act * (root + (root * 0.044715) * squared))
        half = 0.5 * (1.0 + curve)
        activation = (pre_act * half).astype(BF16)
        slope = half + pre_act * (half * (1.0 - curve)) * (root + (3 * root * 0.044715) * squared)
        grad_pre = (slope * (gate * back)).astype(BF16)
        act_ref[0] = activation
        grad_pre_ref[0] = grad_pre
        product = activation.astype(F32) * back
        partial = product[:, :128]
        for low in range(128, product.shape[1], 128):
            partial = partial + product[:, low : low + 128]
        back_sum[...] += partial
        total_ref[...] += mm(grad_pre, weight_in, NT)

    @pl.when(step < steps // 2)
    def _():
        chunk(in_own[0], out_own[0])

    @pl.when(step >= steps // 2)
    def _():
        chunk(in_far[0], out_far[0])

    @pl.when(step == steps - 1)
    def _():
        gate = gate_ref[:, 0:1]
        grad_gate = jnp.sum(back_sum[...], axis=1, keepdims=True)
        signs = logit_ref[...].astype(F32)
        grad_logit = (gate * (1.0 - gate) * grad_gate * signs).astype(BF16)
        logit_ref[...] = grad_logit
        grad_ref[...] = (total_ref[...] + mm(grad_logit, router_ref[...], NT)).astype(grad_ref.dtype)


def expert_pass(own, part, rows, groups, weight, low, local, other, dtype):
    count, width = rows.shape
    units = local[0].shape[2]
    last = 1 if len(local) == 1 else 0
    parts = 2 if units % 256 == 0 else 1
    wide = units // parts
    near = lambda c: jnp.minimum(c, parts - 1)
    far = lambda c: jnp.maximum(c - parts, 0)
    hidden = pl.BlockSpec((1, count, wide), lambda c: (c // parts, 0, c % parts))
    return pl.pallas_call(
        expert_kernel,
        grid=(2 * parts,),
        in_specs=[
            pl.BlockSpec(memory_space=pltpu.SMEM),
            fixed(count, width),
            pl.BlockSpec((1, count, width + 128), lambda c: (part, 0, 0)),
            columns_of(weight, low, 128),
            pl.BlockSpec((1, width, wide), lambda c: (0, 0, near(c))),
            pl.BlockSpec((1, wide, width), lambda c: (last, near(c), 0)),
            pl.BlockSpec((1, width, wide), lambda c: (0, 0, far(c))),
            pl.BlockSpec((1, wide, width), lambda c: (last, far(c), 0)),
        ],
        out_specs=[
            hidden,
            hidden,
            fixed(count, width),
            fixed(count, 128),
            fixed(count, 128),
            fixed(count, width),
        ],
        out_shape=[
            jax.ShapeDtypeStruct((2, count, units), BF16),
            jax.ShapeDtypeStruct((2, count, units), BF16),
            jax.ShapeDtypeStruct((count, width), BF16),
            jax.ShapeDtypeStruct((count, 128), F32),
            jax.ShapeDtypeStruct((count, 128), BF16),
            jax.ShapeDtypeStruct((count, width), dtype),
        ],
        scratch_shapes=[pltpu.VMEM((count, 128), F32), pltpu.VMEM((count, width), F32)],
        cost_estimate=cost(10),
        name="expert_pass",
    )(own[None], rows, groups, weight, local[0], local[-1], other[0], other[-1])


def nesterov(master, momentum, average, grad_full, rate):
    moment_new = MOMENT * momentum + grad_full
    weight_new = master - rate * (grad_full + MOMENT * moment_new)
    return (grad_full, moment_new, weight_new, KEEP_MEAN * average + (1.0 - KEEP_MEAN) * weight_new)


def per_device(
    inputs,
    out_grad,
    seq_lengths,
    routes,
    norm_master,
    norm_momentum,
    norm_average,
    qkv_master,
    qkv_momentum,
    qkv_average,
    proj_master,
    proj_momentum,
    proj_average,
    router_master,
    router_momentum,
    router_average,
    frozen_in,
    frozen_out,
    expert_in_master,
    expert_in_momentum,
    expert_in_average,
    expert_out_master,
    expert_out_momentum,
    expert_out_average,
):
    tok_dev, model_width = inputs.shape
    seq_dev = seq_lengths.shape[0]
    assert seq_dev == 1
    n_expert = lax.axis_size("expert")
    n_hidden = lax.axis_size("hidden")
    experts = 2 * n_expert
    capacity = tok_dev * 2 // experts // 2
    slot_count = experts * capacity
    tokens_all = tok_dev * n_expert * n_hidden
    own_rows = model_width // (n_expert * n_hidden)
    block_rows = min(256, tok_dev)
    qkv_width = 3 * model_width
    expert_index = lax.axis_index("expert")
    hidden_bits = bits_of("hidden")
    weight_bit, token_bits = hidden_bits[0], hidden_bits[1:]

    proj_low, router_low = qkv_width, qkv_width + model_width
    norm_low, whole_width = router_low + 128, router_low + 256
    own_block = jnp.concatenate(
        [
            qkv_master,
            proj_master.T,
            router_master,
            jnp.zeros((own_rows, 128 - experts), F32),
            norm_master.T,
            jnp.zeros((own_rows, 124), F32),
        ],
        axis=1,
    ).astype(BF16)
    far_blocks = gather_far(own_block)

    row_ids = jnp.arange(tok_dev, dtype=jnp.int32)
    live_rows = row_ids < seq_lengths[0]
    live_float = live_rows.astype(F32)[:, None]
    expert_ids = jnp.arange(128, dtype=jnp.int32)
    match = [routes[:, k : k + 1] == expert_ids[None, :] for k in range(2)]
    counts = ((match[0] | match[1]) & live_rows[:, None]).astype(BF16)
    earlier = (row_ids[:, None] > row_ids[None, :]).astype(BF16)
    before = mm(earlier, counts)
    slot_ids = jnp.arange(slot_count, dtype=jnp.int32)
    chosen = None
    for k in range(2):
        rank = jnp.sum(jnp.where(match[k], before, 0.0), axis=1).astype(jnp.int32)
        kept = live_rows & (rank < capacity)
        expert_of = routes[:, k]
        slot = (expert_of % 2 * n_expert + expert_of // 2) * capacity + rank
        hit = jnp.where(kept, slot, -1)[:, None] == slot_ids[None, :]
        chosen = hit if chosen is None else chosen | hit
    select = chosen.astype(BF16)
    route_part = jnp.concatenate(
        [routes.astype(BF16), jnp.zeros((tok_dev, 126), BF16)], axis=1
    )
    grad_out_rows = jnp.where(live_rows[:, None], out_grad, jnp.zeros_like(out_grad))
    early = jnp.concatenate([grad_out_rows, route_part], axis=1)
    early_slots = mm(select, early, TN).astype(BF16)

    far_blocks, early_slots = together(far_blocks, early_slots)
    early_arrived = to_experts(
        early_slots.reshape(2, n_expert, capacity, model_width + 128), 1
    )
    pieces = gather_near(far_blocks, whole_width // 2 // 128 * 128)
    local_weights = [
        bundle(frozen_in[0], frozen_out[0]),
        bundle(expert_in_master[0].astype(BF16), expert_out_master[0].astype(BF16)),
    ]
    parts, sent = together([part for part, _, _ in pieces], local_weights)
    other_weights = [[swap(part, "hidden", weight_bit) for part in some] for some in sent]
    pieces = gather_core([(part, *rest) for part, (_, *rest) in zip(parts, pieces)])

    qkv_rows, attn_in, weights, norm_rows = project_in(
        inputs, pieces, qkv_width, norm_low, whole_width, block_rows
    )
    qkv_rows, early_arrived = together(qkv_rows, early_arrived)
    early_near, early_far = spread(early_arrived.reshape(-1, model_width + 128), token_bits)
    attn_out, log_rows = attend_forward(qkv_rows, seq_lengths, block_rows)
    attn_out, other_weights[0] = together(attn_out, other_weights[0])
    resid_mid, moe_in = project_out(
        inputs, attn_out, norm_rows, weights, proj_low, block_rows
    )

    moe_slots = mm(select, moe_in, TN).astype(BF16)
    moe_slots, early_far = together(moe_slots, early_far)
    moe_slots = moe_slots.reshape(2, n_expert, capacity, model_width)
    spread_rows = n_hidden // 4 if n_hidden > 2 else 1
    group_rows = n_expert * capacity
    early_near, early_far = [
        early.reshape(spread_rows, 2, group_rows, model_width + 128)
        .swapaxes(0, 1)
        .reshape(2, spread_rows * group_rows, model_width + 128)
        for early in (early_near, early_far)
    ]

    def expert(part, rows, groups, dtype):
        *kept, grad = expert_pass(
            2 * expert_index + part,
            part,
            rows.reshape(-1, model_width),
            groups,
            weights,
            router_low,
            local_weights[part],
            other_weights[part],
            dtype,
        )
        return (rows.reshape(-1, model_width), *kept), grad.reshape(rows.shape)

    def home(near, far):
        total = collect(near, far, token_bits)
        return to_experts(total.reshape(n_expert, capacity, model_width)).reshape(-1, model_width)

    near_rows, far_rows = spread(to_experts(moe_slots[0]).reshape(-1, model_width), token_bits)
    near_first, near_grad = expert(0, near_rows, early_near, F32)
    arrived = to_experts(moe_slots[1]).reshape(-1, model_width)
    far_rows, arrived, near_grad = together(far_rows, arrived, near_grad)
    near_rows, next_rows = spread(arrived, token_bits)
    far_first, far_grad = expert(0, far_rows, early_far, BF16)
    near_rows, far_grad = together(near_rows, far_grad)
    far_arrived = swap(far_grad, "hidden", token_bits[-1])
    near_second, next_grad = expert(1, near_rows, early_near, F32)
    next_rows, next_grad = together(next_rows, next_grad)
    far_second, last_grad = expert(1, next_rows, early_far, BF16)
    far_arrived, last_grad = together(far_arrived, last_grad)
    back_first = home(near_grad, far_arrived)
    last_arrived = swap(last_grad, "hidden", token_bits[-1])

    terms = None
    for rows, activation, grad_pre, pair_grad, _, grad_logit in (near_second, far_second):
        activation, grad_pre, grad_logit, last_grad = together(
            activation, grad_pre, grad_logit, last_grad
        )
        new = [mm(rows, grad_pre[k], TN) for k in range(2)]
        new += [mm(activation[k], pair_grad, TN) for k in range(2)]
        terms = new if terms is None else [a + b for a, b in zip(terms, new)]
    away = bundle(terms[1].astype(BF16), terms[3].astype(BF16))
    last_arrived, away = together(last_arrived, away)
    back_second = home(next_grad, last_arrived)
    away = [swap(part, "hidden", weight_bit) for part in away]

    values, router_part = [], 0.0
    for part, (near, far) in enumerate(((near_first, far_first), (near_second, far_second))):
        pair = []
        for rows, activation, grad_pre, pair_grad, gate, grad_logit in (near, far):
            activation, grad_logit, last_arrived = together(activation, grad_logit, last_arrived)
            value = mm(activation[0], local_weights[part][-1][-1])
            value = value + mm(activation[1], other_weights[part][-1][-1])
            pair.append((gate[:, 0:1] * value).reshape(-1, group_rows, model_width))
            router_part = router_part + mm(rows, grad_logit, TN)
        values.append((pair[0], swap(pair[1].astype(BF16), "hidden", token_bits[-1])))
    back_first, back_second, router_part = together(back_first, back_second, router_part)

    grad_mid, grad_branch, grad_attn, row_dot, sums_two = middle_back(
        select, back_first, back_second, resid_mid, grad_out_rows, attn_out, norm_rows, weights,
        proj_low, block_rows
    )
    pairs = HEADS // 2

    def backward(first, count):
        return attend_backward(
            qkv_rows, grad_attn, log_rows, row_dot, seq_lengths, block_rows, first, count
        )

    grads_a = backward(0, pairs // 2)
    far_a, far_b, *grads_a = together(values[0][1], values[1][1], *grads_a)
    values_a = home(values[0][0], far_a)
    split_a = 1024
    sums_a = weight_sums(
        (grad_branch, attn_in), (attn_out, *grads_a), (router_part,), (), split_a, own_rows
    )
    grad_attn, *sums_a = together(grad_attn, *sums_a)
    steps_a = reduce_steps(*sums_a, split_a)
    there_a = next(steps_a)
    grads_b = backward(pairs // 2, pairs // 2 - 1)
    there_a, (grad_attn, values_a, *grads_b) = behind(
        steps_a, there_a, grad_attn, values_a, *grads_b
    )
    values_b = home(values[1][0], far_b)
    grads_c = backward(pairs - 1, 1)
    there_a, grads_c = behind(steps_a, there_a, *grads_c)
    grad_parts = [*grads_a, *grads_b, *grads_c]
    spans = [128 * (first + pairs * k) for first in (0, pairs // 2, pairs - 1) for k in range(3)]
    input_grad, sums_one = last_back(
        inputs, grad_mid, norm_rows, weights, grad_parts, spans, block_rows
    )
    there_a, (sums_one,) = behind(steps_a, there_a, sums_one)
    split_b = 640
    sums_b = weight_sums(
        (attn_in,),
        [part for pair in zip(grads_b, grads_c) for part in pair],
        (),
        (sums_one, sums_two),
        split_b,
        own_rows,
    )
    there_a, sums_b = behind(steps_a, there_a, *sums_b)
    done_a = finish(steps_a, there_a)
    steps_b = reduce_steps(*sums_b, split_b)
    there_b = next(steps_b)
    in_grad = terms[0] + away[0][0].astype(F32)
    out_grad_sum = terms[2] + away[-1][-1].astype(F32)
    done_b = finish(steps_b, there_b)
    outputs = (
        live_float
        * (
            resid_mid
            + mm(select[:, : slot_count // 2], values_a)
            + mm(select[:, slot_count // 2 :], values_b)
        )
    ).astype(BF16)

    proj_sum = done_a[:, :model_width].T
    first_qkv = done_a[:, model_width : model_width + qkv_width // 2]
    router_sum = done_a[:, model_width + qkv_width // 2 :][:, :experts]
    second_qkv = done_b[:, : qkv_width // 2]
    qkv_sum = jnp.concatenate(
        [first_qkv.reshape(own_rows, 3, -1), second_qkv.reshape(own_rows, 3, -1)], axis=2
    ).reshape(own_rows, qkv_width)
    norm_columns = done_b[:, qkv_width // 2 :]
    norm_sum = jnp.concatenate([norm_columns[:, 0:2], norm_columns[:, 8:10]], axis=1).T

    norm_rate = 0.1 / math.sqrt(tokens_all)
    qkv_rate = 1.0 / math.sqrt(model_width * tokens_all)
    proj_rate = 40.0 / math.sqrt(model_width * tokens_all)
    router_rate = 0.08 * math.sqrt(experts / (model_width * tokens_all))
    in_rate = 5.0 * math.sqrt(experts / (model_width * tokens_all))
    out_rate = 2.5 * math.sqrt(experts / (FF * tokens_all))
    norm_set = nesterov(norm_master, norm_momentum, norm_average, norm_sum, norm_rate)
    qkv_set = nesterov(qkv_master, qkv_momentum, qkv_average, qkv_sum, qkv_rate)
    proj_set = nesterov(proj_master, proj_momentum, proj_average, proj_sum, proj_rate)
    router_set = nesterov(router_master, router_momentum, router_average, router_sum, router_rate)
    in_set = nesterov(
        expert_in_master, expert_in_momentum, expert_in_average, in_grad[None], in_rate
    )
    out_set = nesterov(
        expert_out_master, expert_out_momentum, expert_out_average, out_grad_sum[None], out_rate
    )
    return (
        outputs,
        input_grad,
        *norm_set,
        *qkv_set,
        *proj_set,
        *router_set,
        *in_set,
        *out_set,
    )


def solution(mesh):
    rows = P(("expert", "hidden"), None)
    columns = P(None, ("expert", "hidden"))
    expert_in = P("expert", None, "hidden")
    expert_out = P("expert", "hidden", None)
    return jax.shard_map(
        per_device,
        mesh=mesh,
        in_specs=(
            rows,
            rows,
            P(("expert", "hidden")),
            rows,
            *[columns] * 3,
            *[rows] * 3,
            *[columns] * 3,
            *[rows] * 3,
            expert_in,
            expert_out,
            *[expert_in] * 3,
            *[expert_out] * 3,
        ),
        out_specs=(
            rows,
            rows,
            *[columns] * 4,
            *[rows] * 4,
            *[columns] * 4,
            *[rows] * 4,
            *[expert_in] * 4,
            *[expert_out] * 4,
        ),
        check_vma=False,
    )
```
